32 devices in a mesh: row: 8 (over z, x), col: 4 (over y, core).
Axes of the slice: x: 2, y: 2, z: 4, core: 2. Of those that a mesh axis runs over, the one named last changes fastest.
Arguments:
- excitation: bfloat16 [32768, 128], P(('row', 'col')), may hold values from -6 to 6
- near_list: int32 [256, 5], P(('row', 'col')), may hold values from 0 to 255, as said below
- near_blocks: bfloat16 [2, 32768, 640], P(None, ('row', 'col')), may hold values from -0.15625 to 0.15625
- col_factors: bfloat16 [2, 32768, 1024], P(None, ('row', 'col')), may hold values from -0.125 to 0.125
- coupling: bfloat16 [2, 16384, 1024], P(None, ('row', 'col')), may hold values from -0.125 to 0.125
- row_factors: bfloat16 [2, 32768, 512], P(None, ('row', 'col')), may hold values from -0.1875 to 0.1875
Outputs:
- response: bfloat16 [32768, 128], P(('row', 'col'))
The draws below stay inside these ranges and needn't reach their ends.
Inputs may be any that keep to these rules, and one draw needn't show every extreme that they name: near_list[i, 0] = i; every entry lies within 8 leaves of i, and leaves at distance exactly 8 on either side occur.
All inputs are finite; a program needn't handle non-finite values.
Results may differ from the reference program's by a relative error of at most 0.008.
Values may be sent and summed in bfloat16 or wider, within the bound.
No kernel may reach another device: no remote copies, remote signals or barrier semaphores. Data moves between devices by JAX's collectives and lax.ppermute only.
A program may use at most 128 MiB of HBM per device.

```python
import jax
import jax.numpy as jnp
from jax import lax

UNK_DEV = 1024
EXCITE = 64
RANK = 128
LEAF = 128
REACH = 8
NEAR = 5
COLS = 128
UNKNOWNS = 32768
LEAVES = 256
ROW_RANKS = 1024
COL_RANKS = 512
COUPLE_ROWS = 16384
N_ROW = 8
N_COL = 4


def draw_near_list(key, part):
    first_key, second_key = jax.random.split(jax.random.fold_in(key, 17))
    base = jnp.arange(LEAVES, dtype=jnp.int32)[:, None]
    offsets = jax.random.randint(first_key, (LEAVES, NEAR - 2), -REACH, REACH + 1, dtype=jnp.int32)
    direction = jax.random.randint(second_key, (LEAVES, 1), 0, 2, dtype=jnp.int32) * 2 - 1
    steps_all = jnp.concatenate([jnp.zeros((LEAVES, 1), jnp.int32), offsets, direction * REACH], axis=1)
    return jnp.clip(base + steps_all, 0, LEAVES - 1).astype(jnp.int32)


def block_levels(key, dims, shards, least, top_value):
    def one(position, shards_of):
        heights = jax.random.uniform(jax.random.fold_in(jax.random.fold_in(key, 6), position), (shards_of,), jnp.float32, least / len(shards), top_value / len(shards))
        return jnp.repeat(jnp.exp(heights), dims[position] // shards_of).reshape((-1,) + (1,) * (len(dims) - position - 1))

    level = one(*shards[0])
    for cut in shards[1:]:
        level = level * one(*cut)
    return level


def noise(key, shape, deviation, reach, shards=(), kind=jnp.bfloat16):
    gain = block_levels(key, shape, shards, -0.22, 0.18) if shards else 1.0
    result = jax.random.normal(key, shape, jnp.float32) * deviation * gain
    return jnp.minimum(jnp.maximum(result, -reach), reach).astype(kind)


def setup_inputs(seed: int = 0) -> dict:
    seeds = jax.random.split(jax.random.key(seed), 7)
    excitation = noise(seeds[0], (UNKNOWNS, COLS), 1.0, 6.0, ((0, 32),))
    near_list = draw_near_list(jax.random.fold_in(seeds[6], 71), 0)
    near_blocks = noise(seeds[2], (2, UNKNOWNS, NEAR * LEAF), (2 * NEAR * LEAF) ** -0.5, 0.15625, ((1, 32),))
    col_factors = noise(seeds[3], (2, UNKNOWNS, ROW_RANKS), (2 * UNK_DEV) ** -0.5, 0.125, ((1, 32),))
    coupling = noise(seeds[4], (2, COUPLE_ROWS, ROW_RANKS), (2 * ROW_RANKS) ** -0.5, 0.125, ((1, 32),))
    row_factors = noise(seeds[5], (2, UNKNOWNS, COL_RANKS), (2 * COL_RANKS) ** -0.5, 0.1875, ((1, 32),))
    return {"excitation": excitation, "near_list": near_list, "near_blocks": near_blocks, "col_factors": col_factors, "coupling": coupling, "row_factors": row_factors}


def rotate_parts(data, axis):
    real_side = lax.slice_in_dim(data, 0, 1, axis=axis)
    imag_side = lax.slice_in_dim(data, 1, 2, axis=axis)
    return jnp.concatenate([-imag_side, real_side], axis=axis)


def multiply(real_part, imag_part, data):
    count = data.shape[0]
    flattened = data.reshape(count, -1)
    turned = rotate_parts(data, 1).reshape(count, -1)
    summed = jnp.dot(real_part, flattened, preferred_element_type=jnp.float32)
    summed = summed + jnp.dot(imag_part, turned, preferred_element_type=jnp.float32)
    return summed.reshape(real_part.shape[0], 2, -1)


def project(real_part, imag_part, data):
    count = data.shape[0]
    flattened = data.reshape(count, -1)
    turned = rotate_parts(data, 1).reshape(count, -1)
    contract_dims = (((0,), (0,)), ((), ()))
    summed = lax.dot_general(real_part, flattened, contract_dims, preferred_element_type=jnp.float32)
    summed = summed + lax.dot_general(imag_part, turned, contract_dims, preferred_element_type=jnp.float32)
    return summed.reshape(real_part.shape[1], 2, -1)


def multiply_split(real_part, imag_part, data):
    upper_part = data.astype(jnp.bfloat16)
    lower_part = (data - upper_part.astype(jnp.float32)).astype(jnp.bfloat16)
    return multiply(real_part, imag_part, upper_part) + multiply(real_part, imag_part, lower_part)


def reference(excitation, near_list, near_blocks, col_factors, coupling, row_factors):
    clusters = N_ROW * N_COL
    leaves_x = excitation.reshape(LEAVES, LEAF, COLS)
    gathered = leaves_x[near_list].reshape(LEAVES, NEAR * LEAF, 2, EXCITE)
    turned = rotate_parts(gathered, 2).reshape(LEAVES, NEAR * LEAF, COLS)
    gathered = gathered.reshape(LEAVES, NEAR * LEAF, COLS)
    blocks_re = near_blocks[0].reshape(LEAVES, LEAF, NEAR * LEAF).astype(jnp.float32)
    blocks_im = near_blocks[1].reshape(LEAVES, LEAF, NEAR * LEAF).astype(jnp.float32)
    near_field = jnp.einsum("ilm,imc->ilc", blocks_re, gathered.astype(jnp.float32))
    near_field = near_field + jnp.einsum("ilm,imc->ilc", blocks_im, turned.astype(jnp.float32))
    near_field = near_field.reshape(UNKNOWNS, COLS)

    shaped = excitation.reshape(clusters, UNK_DEV, 2, EXCITE)
    vreal = col_factors[0].reshape(clusters, UNK_DEV, ROW_RANKS)
    vimag = col_factors[1].reshape(clusters, UNK_DEV, ROW_RANKS)
    compressed = lax.map(lambda operands: project(operands[0], operands[1], operands[2]), (vreal, vimag, shaped))
    compressed = compressed.reshape(N_ROW, N_COL, N_ROW, RANK, 2, EXCITE).transpose(2, 1, 0, 3, 4, 5)
    arrived = compressed.reshape(clusters, ROW_RANKS, 2, EXCITE)

    breal = coupling[0].reshape(clusters, COL_RANKS, ROW_RANKS)
    bimag = coupling[1].reshape(clusters, COL_RANKS, ROW_RANKS)
    middle = lax.map(lambda operands: multiply_split(operands[0], operands[1], operands[2]), (breal, bimag, arrived))
    middle = middle.reshape(N_ROW, N_COL, N_COL, RANK, 2, EXCITE).transpose(0, 2, 1, 3, 4, 5)
    landed = middle.reshape(clusters, COL_RANKS, 2, EXCITE)

    ureal = row_factors[0].reshape(clusters, UNK_DEV, COL_RANKS)
    uimag = row_factors[1].reshape(clusters, UNK_DEV, COL_RANKS)
    far_field = lax.map(lambda operands: multiply_split(operands[0], operands[1], operands[2]), (ureal, uimag, landed))
    far_field = far_field.reshape(UNKNOWNS, COLS)
    return (near_field + far_field).astype(jnp.bfloat16)
```

```python
import functools

import jax
import jax.numpy as jnp
from jax import lax
from jax.experimental import pallas as pl
from jax.experimental.pallas import tpu as pltpu
from jax.sharding import PartitionSpec as P

RANK = 128
LEAF = 128
REACH = 8
NEAR = 5
MIB = 1 << 20
VMEM = pl.BlockSpec(memory_space=pltpu.VMEM)
SMEM = pl.BlockSpec(memory_space=pltpu.SMEM)
NT = (((1,), (1,)), ((), ()))


def params(mib):
    return pltpu.CompilerParams(vmem_limit_bytes=mib * MIB)


def cost(flops, moved):
    return pl.CostEstimate(flops=flops, bytes_accessed=moved, transcendentals=0)


def dot(a, b):
    return jnp.dot(a, b, preferred_element_type=jnp.float32)


def turn_rows(v):
    half = v.shape[0] // 2
    return jnp.concatenate([-v[half:], v[:half]], axis=0)


def turn_lanes(v):
    half = v.shape[-1] // 2
    rolled = pltpu.roll(v, half, v.ndim - 1)
    lane = lax.broadcasted_iota(jnp.int32, v.shape, v.ndim - 1)
    return jnp.where(lane < half, -rolled, rolled)


def project_kernel(x_ref, v_ref, o_ref, lhs):
    count = x_ref.shape[0]
    turned = x_ref[...].astype(jnp.float32).T.astype(jnp.bfloat16)
    lhs[:, :count] = turned
    lhs[:, count:] = turn_rows(turned)
    groups = o_ref.shape[0]
    step = 2
    for g in range(0, groups, step):
        lanes = slice(g * RANK, (g + step) * RANK)
        total = dot(lhs[:, :count], v_ref[0, :, lanes]) + dot(lhs[:, count:], v_ref[1, :, lanes])
        for s in range(step):
            o_ref[g + s] = total[:, s * RANK : (s + 1) * RANK].astype(jnp.bfloat16)


def project(x, v):
    groups = v.shape[2] // RANK
    count, width = x.shape
    return pl.pallas_call(
        project_kernel,
        out_shape=jax.ShapeDtypeStruct((groups, width, RANK), jnp.bfloat16),
        in_specs=[VMEM, VMEM],
        out_specs=VMEM,
        scratch_shapes=[pltpu.VMEM((width, 2 * count), jnp.bfloat16)],
        compiler_params=params(12),
        cost_estimate=cost(4 * width * v.shape[1] * v.shape[2], v.size * 2),
        name="project",
    )(x, v)


def near_kernel(list_ref, own_ref, first_ref, second_ref, p_ref, o_ref, table, rhs):
    leaves = own_ref.shape[0] // LEAF
    width = own_ref.shape[1]
    here = lax.axis_index(("row", "col"))
    odd = lax.rem(here, 2)
    base = here * leaves
    table[pl.ds(0, leaves)] = own_ref[...].reshape(leaves, LEAF, width)
    table[pl.ds(leaves, leaves)] = first_ref[...].reshape(leaves, LEAF, width)
    table[pl.ds(2 * leaves, leaves)] = second_ref[...].reshape(leaves, LEAF, width)
    for i in range(leaves):
        rows = slice(i * LEAF, (i + 1) * LEAF)
        for j in range(NEAR):
            at = list_ref[i, j] - base
            left = at < 0
            right = at >= leaves
            below = at + leaves * jnp.where(odd == 1, 2, 3)
            above = at + leaves * jnp.where(odd == 1, 1, 0)
            slot = jnp.where(left, below, jnp.where(right, above, at))
            rhs[i % 2, j * LEAF : (j + 1) * LEAF] = table[slot]
        data = rhs[i % 2]
        straight = dot(p_ref[0, rows], data)
        crossed = dot(p_ref[1, rows], data)
        o_ref[rows] = straight + turn_lanes(crossed)


def near(near_list, own, first, second, blocks):
    count, width = own.shape
    leaves = count // LEAF
    return pl.pallas_call(
        near_kernel,
        out_shape=jax.ShapeDtypeStruct((count, width), jnp.float32),
        in_specs=[SMEM, VMEM, VMEM, VMEM, VMEM],
        out_specs=VMEM,
        scratch_shapes=[
            pltpu.VMEM((3 * leaves, LEAF, width), jnp.bfloat16),
            pltpu.VMEM((2, NEAR * LEAF, width), jnp.bfloat16),
        ],
        compiler_params=params(8),
        cost_estimate=cost(4 * width * blocks.shape[1] * blocks.shape[2], blocks.size * 2),
        name="near",
    )(near_list, own, first, second, blocks)


def mid_kernel(a_ref, c_ref, o_ref, rhs):
    groups, width = a_ref.shape[0], a_ref.shape[1]
    for r in range(groups):
        lanes = slice(r * RANK, (r + 1) * RANK)
        rhs[0, :, lanes] = a_ref[r]
        rhs[1, :, lanes] = turn_rows(a_ref[r])
    for k in range(o_ref.shape[0]):
        at = lax.axis_index("col") ^ k
        rows = pl.ds(pl.multiple_of(at * RANK, RANK), RANK)
        total = lax.dot_general(c_ref[0, rows], rhs[0], NT, preferred_element_type=jnp.float32)
        total += lax.dot_general(c_ref[1, rows], rhs[1], NT, preferred_element_type=jnp.float32)
        o_ref[k] = total.astype(jnp.bfloat16)


def mid(arrived, coupling):
    groups, width, _ = arrived.shape
    blocks = coupling.shape[1] // RANK
    return pl.pallas_call(
        mid_kernel,
        out_shape=jax.ShapeDtypeStruct((blocks, RANK, width), jnp.bfloat16),
        in_specs=[VMEM, VMEM],
        out_specs=VMEM,
        scratch_shapes=[pltpu.VMEM((2, width, groups * RANK), jnp.bfloat16)],
        compiler_params=params(8),
        cost_estimate=cost(4 * width * coupling.shape[1] * coupling.shape[2], coupling.size * 2),
        name="mid",
    )(arrived, coupling)


def far_kernel(*refs):
    *landed, u_ref, n_ref, o_ref, data, crossed = refs
    blocks = len(landed)
    for k in range(blocks):
        at = lax.axis_index("col") ^ k
        rows = pl.ds(pl.multiple_of(at * RANK, RANK), RANK)
        value = landed[k][...]
        data[rows] = value
        crossed[rows] = turn_lanes(value.astype(jnp.float32)).astype(jnp.bfloat16)
    step = 256
    for i in range(0, o_ref.shape[0], step):
        rows = slice(i, i + step)
        total = dot(u_ref[0, rows], data[...]) + dot(u_ref[1, rows], crossed[...])
        o_ref[rows] = (total + n_ref[rows]).astype(jnp.bfloat16)


def far(landed, factors, near_field):
    count, width = near_field.shape
    ranks = len(landed) * RANK
    return pl.pallas_call(
        far_kernel,
        out_shape=jax.ShapeDtypeStruct((count, width), jnp.bfloat16),
        in_specs=[VMEM] * (len(landed) + 2),
        out_specs=VMEM,
        scratch_shapes=[pltpu.VMEM((ranks, width), jnp.bfloat16)] * 2,
        compiler_params=params(8),
        cost_estimate=cost(4 * width * factors.shape[1] * factors.shape[2], factors.size * 2),
        name="far",
    )(*landed, factors, near_field)


def on_device(excitation, near_list, near_blocks, col_factors, coupling, row_factors):
    row_count = lax.axis_size("row")
    col_count = lax.axis_size("col")
    total = row_count * col_count
    axes = ("row", "col")
    inner = [(i, i ^ 1) for i in range(total)]
    outer = [(i, ((i + 1) ^ 1) - 1) for i in range(1, total - 1)]
    second = lax.ppermute(excitation, axes, outer)
    first = lax.ppermute(excitation, axes, inner)
    compressed = project(excitation, col_factors)
    arrived = lax.all_to_all(compressed, "row", split_axis=0, concat_axis=0, tiled=True)
    near_field = near(near_list, excitation, first, second, near_blocks)
    middle = mid(arrived, coupling)
    landed = [middle[0]]
    for k in range(1, col_count):
        landed.append(lax.ppermute(middle[k], "col", [(i, i ^ k) for i in range(col_count)]))
    return far(landed, row_factors, near_field)


def solution(mesh):
    return jax.shard_map(
        on_device,
        mesh=mesh,
        in_specs=(
            P(("row", "col"), None),
            P(("row", "col"), None),
            P(None, ("row", "col"), None),
            P(None, ("row", "col"), None),
            P(None, ("row", "col"), None),
            P(None, ("row", "col"), None),
        ),
        out_specs=P(("row", "col"), None),
        check_vma=False,
    )
```

```python
import functools

import jax
import jax.numpy as jnp
from jax import lax
from jax.experimental import pallas as pl
from jax.experimental.pallas import tpu as pltpu
from jax.sharding import PartitionSpec as P

RANK = 128
LEAF = 128
NEAR = 5
MIB = 1 << 20
VMEM = pl.BlockSpec(memory_space=pltpu.VMEM)
HBM = pl.BlockSpec(memory_space=pltpu.HBM)
SMEM = pl.BlockSpec(memory_space=pltpu.SMEM)
NT = (((1,), (1,)), ((), ()))


def params(mib):
    return pltpu.CompilerParams(vmem_limit_bytes=mib * MIB)


def cost(flops, moved):
    return pl.CostEstimate(flops=flops, bytes_accessed=moved, transcendentals=0)


def dot(a, b):
    return jnp.dot(a, b, preferred_element_type=jnp.float32)


def turn_rows(v):
    half = v.shape[0] // 2
    return jnp.concatenate([-v[half:], v[:half]], axis=0)


def turn_lanes(v):
    half = v.shape[-1] // 2
    rolled = pltpu.roll(v, half, v.ndim - 1)
    lane = lax.broadcasted_iota(jnp.int32, v.shape, v.ndim - 1)
    return jnp.where(lane < half, -rolled, rolled)


def project_kernel(x_hbm, v_hbm, o_hbm, x_ref, v_ref, lhs, part, o_ref, x_sem, v_sem, o_sem):
    half = x_ref.shape[0] // 2
    wide = 2 * RANK
    pieces = v_ref.shape[2] // wide

    def fetch(k, p):
        rows = pl.ds(k * half, half)
        return pltpu.make_async_copy(v_hbm.at[p, rows], v_ref.at[p, rows], v_sem.at[k, p])

    def leave(n):
        rows = pl.ds(n * 2, 2)
        return pltpu.make_async_copy(o_ref.at[rows], o_hbm.at[rows], o_sem.at[n])

    def product(k, n):
        rows = slice(k * half, (k + 1) * half)
        lanes = slice(n * wide, (n + 1) * wide)
        return dot(lhs[0, :, rows], v_ref[0, rows, lanes]) + dot(lhs[1, :, rows], v_ref[1, rows, lanes])

    load = pltpu.make_async_copy(x_hbm, x_ref, x_sem)
    load.start()
    for k in range(2):
        for p in range(2):
            fetch(k, p).start()
    load.wait()
    turned = x_ref[...].astype(jnp.float32).T.astype(jnp.bfloat16)
    lhs[0] = turned
    lhs[1] = turn_rows(turned)
    for p in range(2):
        fetch(0, p).wait()
    for n in range(pieces):
        part[n] = product(0, n)
    for p in range(2):
        fetch(1, p).wait()
    for n in range(pieces):
        total = part[n] + product(1, n)
        for s in range(2):
            o_ref[n * 2 + s] = total[:, s * RANK : (s + 1) * RANK].astype(jnp.bfloat16)
        leave(n).start()
    for n in range(pieces):
        leave(n).wait()


def project(x, v):
    groups = v.shape[2] // RANK
    count, width = x.shape
    return pl.pallas_call(
        project_kernel,
        out_shape=jax.ShapeDtypeStruct((groups, width, RANK), jnp.bfloat16),
        in_specs=[HBM, HBM],
        out_specs=HBM,
        scratch_shapes=[
            pltpu.VMEM(x.shape, x.dtype),
            pltpu.VMEM(v.shape, v.dtype),
            pltpu.VMEM((2, width, count), v.dtype),
            pltpu.VMEM((groups // 2, width, 2 * RANK), jnp.float32),
            pltpu.VMEM((groups, width, RANK), v.dtype),
            pltpu.SemaphoreType.DMA(()),
            pltpu.SemaphoreType.DMA((2, 2)),
            pltpu.SemaphoreType.DMA((groups // 2,)),
        ],
        compiler_params=params(60),
        cost_estimate=cost(4 * width * v.shape[1] * v.shape[2], v.size * 2),
        name="project",
    )(x, v)


def slots_kernel(list_ref, o_ref):
    leaves = list_ref.shape[0]
    here = lax.axis_index(("row", "col"))
    odd = lax.rem(here, 2)
    at = list_ref[...] - here * leaves
    below = at + leaves * jnp.where(odd == 1, 2, 3)
    above = at + leaves * jnp.where(odd == 1, 1, 0)
    o_ref[...] = jnp.where(at < 0, below, jnp.where(at >= leaves, above, at))


def slots_of(near_list):
    return pl.pallas_call(
        slots_kernel,
        out_shape=jax.ShapeDtypeStruct(near_list.shape, jnp.int32),
        in_specs=[VMEM],
        out_specs=VMEM,
        compiler_params=params(1),
        cost_estimate=cost(10**10, near_list.size * 8),
        name="slots",
    )(near_list)


def near_kernel(slot_ref, own_ref, first_ref, second_ref, p_ref, o_ref, table, rhs):
    leaves = own_ref.shape[0] // LEAF
    width = own_ref.shape[1]
    for n, ref in enumerate((own_ref, first_ref, second_ref)):
        table[pl.ds(n * leaves, leaves)] = ref[...].reshape(leaves, LEAF, width)
    for i in range(leaves):
        rows = slice(i * LEAF, (i + 1) * LEAF)
        for j in range(NEAR):
            rhs[i % 2, j * LEAF : (j + 1) * LEAF] = table[slot_ref[i, j]]
        data = rhs[i % 2]
        straight = dot(p_ref[0, rows], data)
        crossed = dot(p_ref[1, rows], data)
        o_ref[rows] = straight + turn_lanes(crossed)


def near(slots, own, first, second, blocks):
    count, width = own.shape
    leaves = count // LEAF
    return pl.pallas_call(
        near_kernel,
        out_shape=jax.ShapeDtypeStruct((count, width), jnp.float32),
        in_specs=[SMEM, VMEM, VMEM, VMEM, VMEM],
        out_specs=VMEM,
        scratch_shapes=[
            pltpu.VMEM((3 * leaves, LEAF, width), jnp.bfloat16),
            pltpu.VMEM((2, NEAR * LEAF, width), jnp.bfloat16),
        ],
        compiler_params=params(4),
        cost_estimate=cost(4 * width * blocks.shape[1] * blocks.shape[2], blocks.size * 2),
        name="near",
    )(slots, own, first, second, blocks)


def mid_kernel(hops, a_ref, c_ref, *refs):
    *outs, rhs = refs
    for r in range(a_ref.shape[0]):
        lanes = slice(r * RANK, (r + 1) * RANK)
        rhs[0, :, lanes] = a_ref[r]
        rhs[1, :, lanes] = turn_rows(a_ref[r])
    for k, o_ref in zip(hops, outs):
        at = lax.axis_index("col") ^ k
        rows = pl.ds(pl.multiple_of(at * RANK, RANK), RANK)
        total = lax.dot_general(c_ref[0, rows], rhs[0], NT, preferred_element_type=jnp.float32)
        total += lax.dot_general(c_ref[1, rows], rhs[1], NT, preferred_element_type=jnp.float32)
        o_ref[...] = total.astype(jnp.bfloat16)


def mid(hops, arrived, coupling):
    groups, width, _ = arrived.shape
    share = len(hops) * RANK * coupling.shape[2]
    return pl.pallas_call(
        functools.partial(mid_kernel, hops),
        out_shape=[jax.ShapeDtypeStruct((RANK, width), jnp.bfloat16)] * len(hops),
        in_specs=[VMEM, VMEM],
        out_specs=[VMEM] * len(hops),
        scratch_shapes=[pltpu.VMEM((2, width, groups * RANK), jnp.bfloat16)],
        compiler_params=params(4),
        cost_estimate=cost(4 * width * share, share * 4),
        name="mid",
    )(arrived, coupling)


def far_kernel(hops, *refs):
    landed, (u_ref, n_ref, o_ref, data) = refs[: len(hops)], refs[len(hops) :]
    me = lax.axis_index("col")
    for n, k in enumerate(hops):
        at = pl.ds(pl.multiple_of((n & ~1) * RANK + ((me ^ k) & 1) * RANK, RANK), RANK)
        value = landed[n][...]
        data[0, at] = value
        data[1, at] = turn_lanes(value.astype(jnp.float32)).astype(jnp.bfloat16)
    step = 2 * RANK
    for i in range(0, n_ref.shape[0], step):
        rows = slice(i, i + step)
        total = n_ref[rows]
        for n in range(0, len(hops), 2):
            lanes = pl.ds(pl.multiple_of(((me ^ hops[n]) & ~1) * RANK, 2 * RANK), 2 * RANK)
            at = slice(n * RANK, (n + 2) * RANK)
            total += dot(u_ref[0, rows, lanes], data[0, at]) + dot(u_ref[1, rows, lanes], data[1, at])
        o_ref[rows] = total.astype(o_ref.dtype)


def far(hops, landed, factors, near_field, kind):
    count, width = near_field.shape
    share = len(hops) * RANK * count
    return pl.pallas_call(
        functools.partial(far_kernel, hops),
        out_shape=jax.ShapeDtypeStruct((count, width), kind),
        in_specs=[VMEM] * (len(hops) + 2),
        out_specs=VMEM,
        scratch_shapes=[pltpu.VMEM((2, len(hops) * RANK, width), jnp.bfloat16)],
        compiler_params=params(4),
        cost_estimate=cost(4 * width * share, share * 4),
        name="far",
    )(*landed, factors, near_field)


def stages(excitation, near_list, near_blocks, col_factors, coupling, row_factors):
    row_count = lax.axis_size("row")
    col_count = lax.axis_size("col")
    total = row_count * col_count
    axes = ("row", "col")
    inner = [(i, i ^ 1) for i in range(total)]
    outer = [(i, ((i + 1) ^ 1) - 1) for i in range(1, total - 1)]
    second = lax.ppermute(excitation, axes, outer)
    first = lax.ppermute(excitation, axes, inner)
    compressed = project(excitation, col_factors)
    arrived = lax.all_to_all(compressed, "row", split_axis=0, concat_axis=0, tiled=True)
    slots = slots_of(near_list)
    early = list(range(2, col_count))
    late = [1, 0]
    sent = dict(zip(early, mid(early, arrived, coupling)))
    sent.update(zip(late, mid(late, arrived, coupling)))
    landed = {0: sent[0]}
    for k in reversed(range(1, col_count)):
        landed[k] = lax.ppermute(sent[k], "col", [(i, i ^ k) for i in range(col_count)])
    total = near(slots, excitation, first, second, near_blocks)
    total = far([0, 1], [landed[0], landed[1]], row_factors, total, jnp.float32)
    return far(early, [landed[k] for k in early], row_factors, total, jnp.bfloat16)


def solution(mesh):
    return jax.shard_map(
        stages,
        mesh=mesh,
        in_specs=(
            P(("row", "col"), None),
            P(("row", "col"), None),
            P(None, ("row", "col"), None),
            P(None, ("row", "col"), None),
            P(None, ("row", "col"), None),
            P(None, ("row", "col"), None),
        ),
        out_specs=P(("row", "col"), None),
        check_vma=False,
    )
```

```python
import functools

import jax
import jax.numpy as jnp
from jax import lax
from jax.experimental import pallas as pl
from jax.experimental.pallas import tpu as pltpu
from jax.sharding import PartitionSpec as P

RANK = 128
LEAF = 128
NEAR = 5
MIB = 1 << 20
VMEM = pl.BlockSpec(memory_space=pltpu.VMEM)
HBM = pl.BlockSpec(memory_space=pltpu.HBM)
SMEM = pl.BlockSpec(memory_space=pltpu.SMEM)
NT = (((1,), (1,)), ((), ()))


def params(mib):
    return pltpu.CompilerParams(vmem_limit_bytes=int(mib * MIB))


def cost(flops, moved):
    return pl.CostEstimate(flops=flops, bytes_accessed=moved, transcendentals=0)


def dot(a, b):
    return jnp.dot(a, b, preferred_element_type=jnp.float32)


def turn_rows(v):
    half = v.shape[0] // 2
    return jnp.concatenate([-v[half:], v[:half]], axis=0)


def turn_lanes(v):
    half = v.shape[-1] // 2
    rolled = pltpu.roll(v, half, v.ndim - 1)
    lane = lax.broadcasted_iota(jnp.int32, v.shape, v.ndim - 1)
    return jnp.where(lane < half, -rolled, rolled)


def project_kernel(x_hbm, v_hbm, own_ref, cross_ref, x_ref, v_ref, lhs, part, x_sem, v_sem):
    row = lax.axis_index("row")
    half = x_ref.shape[0] // 2
    wide = 2 * RANK
    pieces = v_ref.shape[2] // wide

    def fetch(k, p):
        rows = pl.ds(k * half, half)
        return pltpu.make_async_copy(v_hbm.at[p, rows], v_ref.at[p, rows], v_sem.at[k, p])

    def product(k, n):
        rows = slice(k * half, (k + 1) * half)
        lanes = slice(n * wide, (n + 1) * wide)
        return dot(lhs[0, :, rows], v_ref[0, rows, lanes]) + dot(lhs[1, :, rows], v_ref[1, rows, lanes])

    load = pltpu.make_async_copy(x_hbm, x_ref, x_sem)
    load.start()
    for k in range(2):
        for p in range(2):
            fetch(k, p).start()
    load.wait()
    turned = x_ref[...].astype(jnp.float32).T.astype(jnp.bfloat16)
    lhs[0] = turned
    lhs[1] = turn_rows(turned)
    for p in range(2):
        fetch(0, p).wait()
    for n in range(pieces):
        part[n] = product(0, n)
    for p in range(2):
        fetch(1, p).wait()
    for n in range(pieces):
        total = (part[n] + product(1, n)).astype(jnp.bfloat16)
        first, second = total[:, :RANK], total[:, RANK:]
        at = n ^ (row // 2)
        own_ref[at] = jnp.where(row % 2 == 0, first, second)
        cross_ref[at] = jnp.where(row % 2 == 0, second, first)


def project(x, v):
    groups = v.shape[2] // RANK
    count, width = x.shape
    return pl.pallas_call(
        project_kernel,
        out_shape=[jax.ShapeDtypeStruct((groups // 2, width, RANK), jnp.bfloat16)] * 2,
        in_specs=[HBM, HBM],
        out_specs=[VMEM, VMEM],
        scratch_shapes=[
            pltpu.VMEM(x.shape, x.dtype),
            pltpu.VMEM(v.shape, v.dtype),
            pltpu.VMEM((2, width, count), v.dtype),
            pltpu.VMEM((groups // 2, width, 2 * RANK), jnp.float32),
            pltpu.SemaphoreType.DMA(()),
            pltpu.SemaphoreType.DMA((2, 2)),
        ],
        compiler_params=params(53.6),
        cost_estimate=cost(4 * width * v.shape[1] * v.shape[2], v.size * 2),
        name="project",
    )(x, v)


def slots_kernel(list_ref, o_ref):
    leaves = list_ref.shape[0]
    here = lax.axis_index(("row", "col"))
    odd = lax.rem(here, 2)
    at = list_ref[...] - here * leaves
    below = at + leaves * jnp.where(odd == 1, 2, 3)
    above = at + leaves * jnp.where(odd == 1, 1, 0)
    o_ref[...] = jnp.where(at < 0, below, jnp.where(at >= leaves, above, at))


def slots_of(near_list):
    return pl.pallas_call(
        slots_kernel,
        out_shape=jax.ShapeDtypeStruct(near_list.shape, jnp.int32),
        in_specs=[VMEM],
        out_specs=VMEM,
        compiler_params=params(1),
        cost_estimate=cost(10**10, near_list.size * 8),
        name="slots",
    )(near_list)


def near_kernel(slot_ref, own_ref, first_ref, second_ref, third_ref, p_ref, o_ref, table, rhs):
    leaves = own_ref.shape[0] // LEAF
    width = own_ref.shape[1]
    for n, ref in enumerate((own_ref, first_ref)):
        table[pl.ds(n * leaves, leaves)] = ref[...].reshape(leaves, LEAF, width)
    col = lax.axis_index("col")
    edge = (col == 0) | (col == lax.axis_size("col") - 1)

    @pl.when(edge)
    def _():
        table[pl.ds(2 * leaves, leaves)] = third_ref[...].reshape(leaves, LEAF, width)

    @pl.when(jnp.logical_not(edge))
    def _():
        table[pl.ds(2 * leaves, leaves)] = second_ref[...].reshape(leaves, LEAF, width)

    for i in range(leaves):
        rows = slice(i * LEAF, (i + 1) * LEAF)
        for j in range(NEAR):
            rhs[i % 2, j * LEAF : (j + 1) * LEAF] = table[slot_ref[i, j]]
        data = rhs[i % 2]
        straight = dot(p_ref[0, rows], data)
        crossed = dot(p_ref[1, rows], data)
        o_ref[rows] = straight + turn_lanes(crossed)


def near(slots, own, first, second, third, blocks):
    count, width = own.shape
    leaves = count // LEAF
    return pl.pallas_call(
        near_kernel,
        out_shape=jax.ShapeDtypeStruct((count, width), jnp.float32),
        in_specs=[SMEM] + [VMEM] * 5,
        out_specs=VMEM,
        scratch_shapes=[
            pltpu.VMEM((3 * leaves, LEAF, width), jnp.bfloat16),
            pltpu.VMEM((2, NEAR * LEAF, width), jnp.bfloat16),
        ],
        compiler_params=params(4),
        cost_estimate=cost(4 * width * blocks.shape[1] * blocks.shape[2], blocks.size * 2),
        name="near",
    )(slots, own, first, second, third, blocks)


def pack_kernel(own_ref, got_ref, *outs):
    for k, o_ref in enumerate(outs):
        o_ref[0] = own_ref[k + 1]
        o_ref[1] = got_ref[k + 1]


def pack(own, got):
    count = own.shape[0] - 1
    return pl.pallas_call(
        pack_kernel,
        out_shape=[jax.ShapeDtypeStruct((2, *own.shape[1:]), own.dtype)] * count,
        in_specs=[VMEM, VMEM],
        out_specs=[VMEM] * count,
        compiler_params=params(1),
        cost_estimate=cost(0, own.size * 8),
        name="pack",
    )(own, got)


def mid_kernel(hops, own_ref, got_ref, *refs):
    half = own_ref.shape[0]
    arrived, c_ref, outs, rhs = refs[: half - 1], refs[half - 1], refs[half:-1], refs[-1]
    row = lax.axis_index("row")
    for k in range(2 * half):
        at = pl.ds(pl.multiple_of((row ^ k) * RANK, RANK), RANK)
        if k < 2:
            value = (own_ref, got_ref)[k][0]
        else:
            value = arrived[k // 2 - 1][k % 2]
        rhs[0, :, at] = value
        rhs[1, :, at] = turn_rows(value)
    for k, o_ref in zip(hops, outs):
        at = lax.axis_index("col") ^ k
        rows = pl.ds(pl.multiple_of(at * RANK, RANK), RANK)
        total = lax.dot_general(c_ref[0, rows], rhs[0], NT, preferred_element_type=jnp.float32)
        total += lax.dot_general(c_ref[1, rows], rhs[1], NT, preferred_element_type=jnp.float32)
        o_ref[...] = total.astype(jnp.bfloat16)


def mid(hops, own, got, arrived, coupling):
    half, width, _ = own.shape
    share = len(hops) * RANK * coupling.shape[2]
    return pl.pallas_call(
        functools.partial(mid_kernel, hops),
        out_shape=[jax.ShapeDtypeStruct((RANK, width), jnp.bfloat16)] * len(hops),
        in_specs=[VMEM] * (half + 2),
        out_specs=[VMEM] * len(hops),
        scratch_shapes=[pltpu.VMEM((2, width, 2 * half * RANK), jnp.bfloat16)],
        compiler_params=params(4),
        cost_estimate=cost(4 * width * share, share * 4),
        name="mid",
    )(own, got, *arrived, coupling)


def far_kernel(hops, *refs):
    landed, (u_ref, n_ref, o_ref, data) = refs[: len(hops)], refs[len(hops) :]
    me = lax.axis_index("col")
    for n, k in enumerate(hops):
        at = pl.ds(pl.multiple_of((n & ~1) * RANK + ((me ^ k) & 1) * RANK, RANK), RANK)
        value = landed[n][...]
        data[0, at] = value
        data[1, at] = turn_lanes(value.astype(jnp.float32)).astype(jnp.bfloat16)
    step = 2 * RANK
    for i in range(0, n_ref.shape[0], step):
        rows = slice(i, i + step)
        total = n_ref[rows]
        for n in range(0, len(hops), 2):
            lanes = pl.ds(pl.multiple_of(((me ^ hops[n]) & ~1) * RANK, 2 * RANK), 2 * RANK)
            at = slice(n * RANK, (n + 2) * RANK)
            total += dot(u_ref[0, rows, lanes], data[0, at]) + dot(u_ref[1, rows, lanes], data[1, at])
        o_ref[rows] = total.astype(o_ref.dtype)


def far(hops, landed, factors, near_field, kind):
    count, width = near_field.shape
    share = len(hops) * RANK * count
    return pl.pallas_call(
        functools.partial(far_kernel, hops),
        out_shape=jax.ShapeDtypeStruct((count, width), kind),
        in_specs=[VMEM] * (len(hops) + 2),
        out_specs=VMEM,
        scratch_shapes=[pltpu.VMEM((2, len(hops) * RANK, width), jnp.bfloat16)],
        compiler_params=params(4),
        cost_estimate=cost(4 * width * share, share * 4),
        name="far",
    )(*landed, factors, near_field)


def stages(excitation, near_list, near_blocks, col_factors, coupling, row_factors):
    row_count = lax.axis_size("row")
    col_count = lax.axis_size("col")
    total = row_count * col_count
    axes = ("row", "col")
    inner = [(i, i ^ 1) for i in range(total)]
    outer, edge = [], []
    for i in range(1, total - 1):
        j = ((i + 1) ^ 1) - 1
        (outer if i // col_count == j // col_count else edge).append((i, j))
    third = lax.ppermute(excitation, axes, edge)
    second = lax.ppermute(excitation, axes, outer)
    first = lax.ppermute(excitation, axes, inner)
    own, cross = project(excitation, col_factors)
    got = lax.ppermute(cross, "row", [(i, i ^ 1) for i in range(row_count)])
    sent = pack(own, got)
    arrived = []
    for k in range(1, row_count // 2):
        arrived.append(lax.ppermute(sent[k - 1], "row", [(i, i ^ (2 * k)) for i in range(row_count)]))
    slots = slots_of(near_list)
    early = list(range(2, col_count))
    late = [1, 0]
    sent = dict(zip(early, mid(early, own, got, arrived, coupling)))
    sent.update(zip(late, mid(late, own, got, arrived, coupling)))
    landed = {0: sent[0]}
    for k in reversed(range(1, col_count)):
        landed[k] = lax.ppermute(sent[k], "col", [(i, i ^ k) for i in range(col_count)])
    total = near(slots, excitation, first, second, third, near_blocks)
    total = far([0, 1], [landed[0], landed[1]], row_factors, total, jnp.float32)
    return far(early, [landed[k] for k in early], row_factors, total, jnp.bfloat16)


def solution(mesh):
    return jax.shard_map(
        stages,
        mesh=mesh,
        in_specs=(
            P(("row", "col"), None),
            P(("row", "col"), None),
            P(None, ("row", "col"), None),
            P(None, ("row", "col"), None),
            P(None, ("row", "col"), None),
            P(None, ("row", "col"), None),
        ),
        out_specs=P(("row", "col"), None),
        check_vma=False,
    )
```

```python
import functools

import jax
import jax.numpy as jnp
from jax import lax
from jax.experimental import pallas as pl
from jax.experimental.pallas import tpu as pltpu
from jax.sharding import PartitionSpec as P

RANK = 128
LEAF = 128
NEAR = 5
MIB = 1 << 20
VMEM = pl.BlockSpec(memory_space=pltpu.VMEM)
HBM = pl.BlockSpec(memory_space=pltpu.HBM)
SMEM = pl.BlockSpec(memory_space=pltpu.SMEM)
NT = (((1,), (1,)), ((), ()))


def params(mib):
    return pltpu.CompilerParams(vmem_limit_bytes=int(mib * MIB))


def cost(flops, moved):
    return pl.CostEstimate(flops=flops, bytes_accessed=moved, transcendentals=0)


def dot(a, b):
    return jnp.dot(a, b, preferred_element_type=jnp.float32)


def turn_rows(v):
    half = v.shape[0] // 2
    return jnp.concatenate([-v[half:], v[:half]], axis=0)


def turn_lanes(v):
    half = v.shape[-1] // 2
    rolled = pltpu.roll(v, half, v.ndim - 1)
    lane = lax.broadcasted_iota(jnp.int32, v.shape, v.ndim - 1)
    return jnp.where(lane < half, -rolled, rolled)


def project_kernel(x_hbm, v_hbm, own_ref, cross_ref, x_ref, v_ref, lhs, part, x_sem, v_sem):
    row = lax.axis_index("row")
    half = x_ref.shape[0] // 2
    wide = 2 * RANK
    pieces = v_ref.shape[2] // wide

    def fetch(k, p):
        rows = pl.ds(k * half, half)
        return pltpu.make_async_copy(v_hbm.at[p, rows], v_ref.at[p, rows], v_sem.at[k, p])

    def product(k, n):
        rows = slice(k * half, (k + 1) * half)
        lanes = slice(n * wide, (n + 1) * wide)
        return dot(lhs[0, :, rows], v_ref[0, rows, lanes]) + dot(lhs[1, :, rows], v_ref[1, rows, lanes])

    load = pltpu.make_async_copy(x_hbm, x_ref, x_sem)
    load.start()
    for k in range(2):
        for p in range(2):
            fetch(k, p).start()
    load.wait()
    turned = x_ref[...].astype(jnp.float32).T.astype(jnp.bfloat16)
    lhs[0] = turned
    lhs[1] = turn_rows(turned)
    for p in range(2):
        fetch(0, p).wait()
    for n in range(pieces):
        part[n] = product(0, n)
    for p in range(2):
        fetch(1, p).wait()
    for n in range(pieces):
        total = (part[n] + product(1, n)).astype(jnp.bfloat16)
        first, second = total[:, :RANK], total[:, RANK:]
        at = n ^ (row // 2)
        own_ref[at] = jnp.where(row % 2 == 0, first, second)
        cross_ref[at] = jnp.where(row % 2 == 0, second, first)


def project(x, v):
    groups = v.shape[2] // RANK
    count, width = x.shape
    return pl.pallas_call(
        project_kernel,
        out_shape=[jax.ShapeDtypeStruct((groups // 2, width, RANK), jnp.bfloat16)] * 2,
        in_specs=[HBM, HBM],
        out_specs=[VMEM, VMEM],
        scratch_shapes=[
            pltpu.VMEM(x.shape, x.dtype),
            pltpu.VMEM(v.shape, v.dtype),
            pltpu.VMEM((2, width, count), v.dtype),
            pltpu.VMEM((groups // 2, width, 2 * RANK), jnp.float32),
            pltpu.SemaphoreType.DMA(()),
            pltpu.SemaphoreType.DMA((2, 2)),
        ],
        compiler_params=params(53.6),
        cost_estimate=cost(4 * width * v.shape[1] * v.shape[2], v.size * 2),
        name="project",
    )(x, v)


def slots_kernel(list_ref, o_ref):
    leaves = list_ref.shape[0]
    here = lax.axis_index(("row", "col"))
    odd = lax.rem(here, 2)
    at = list_ref[...] - here * leaves
    below = at + leaves * jnp.where(odd == 1, 2, 3)
    above = at + leaves * jnp.where(odd == 1, 1, 0)
    o_ref[...] = jnp.where(at < 0, below, jnp.where(at >= leaves, above, at))


def slots_of(near_list):
    return pl.pallas_call(
        slots_kernel,
        out_shape=jax.ShapeDtypeStruct(near_list.shape, jnp.int32),
        in_specs=[VMEM],
        out_specs=VMEM,
        compiler_params=params(1),
        cost_estimate=cost(10**10, near_list.size * 8),
        name="slots",
    )(near_list)


def table_kernel(own_ref, first_ref, o_ref):
    count = own_ref.shape[0]
    o_ref[:count] = own_ref[...]
    o_ref[count : 2 * count] = first_ref[...]


def table_of(own, first):
    count, width = own.shape
    return pl.pallas_call(
        table_kernel,
        out_shape=jax.ShapeDtypeStruct((3 * count, width), own.dtype),
        in_specs=[VMEM, VMEM],
        out_specs=VMEM,
        compiler_params=params(1),
        cost_estimate=cost(0, own.size * 8),
        name="table",
    )(own, first)


def near_kernel(slot_ref, table_in, second_ref, third_ref, p_ref, o_ref, table, rhs):
    count = second_ref.shape[0]
    col = lax.axis_index("col")
    edge = (col == 0) | (col == lax.axis_size("col") - 1)

    @pl.when(edge)
    def _():
        table[2 * count :] = third_ref[...]

    @pl.when(jnp.logical_not(edge))
    def _():
        table[2 * count :] = second_ref[...]

    slots = slot_ref[...] * LEAF
    for i in range(count // LEAF):
        rows = slice(i * LEAF, (i + 1) * LEAF)
        for j in range(NEAR):
            at = pl.ds(pl.multiple_of(slots[i, j], LEAF), LEAF)
            rhs[i % 2, j * LEAF : (j + 1) * LEAF] = table[at]
        data = rhs[i % 2]
        straight = dot(p_ref[0, rows], data)
        crossed = dot(p_ref[1, rows], data)
        o_ref[rows] = straight + turn_lanes(crossed)


def near(slots, table, second, third, blocks):
    count, width = second.shape
    return pl.pallas_call(
        near_kernel,
        out_shape=[
            jax.ShapeDtypeStruct((count, width), jnp.float32),
            jax.ShapeDtypeStruct(table.shape, table.dtype),
        ],
        in_specs=[VMEM] * 5,
        out_specs=[VMEM, VMEM],
        input_output_aliases={1: 1},
        scratch_shapes=[pltpu.VMEM((2, NEAR * LEAF, width), jnp.bfloat16)],
        compiler_params=params(4),
        cost_estimate=cost(4 * width * blocks.shape[1] * blocks.shape[2], blocks.size * 2),
        name="near",
    )(slots, table, second, third, blocks)[0]


def pack_kernel(hops, own_ref, got_ref, *outs):
    base = hops[-1] + 1 - got_ref.shape[0]
    for k, o_ref in zip(hops, outs):
        o_ref[0] = own_ref[k]
        o_ref[1] = got_ref[k - base]


def pack(hops, own, got):
    return pl.pallas_call(
        functools.partial(pack_kernel, hops),
        out_shape=[jax.ShapeDtypeStruct((2, *own.shape[1:]), own.dtype)] * len(hops),
        in_specs=[VMEM, VMEM],
        out_specs=[VMEM] * len(hops),
        compiler_params=params(1),
        cost_estimate=cost(0, len(hops) * own.size * 2),
        name="pairs",
    )(own, got)


def couple(hops, c_ref, rhs, outs):
    for k, o_ref in zip(hops, outs):
        at = lax.axis_index("col") ^ k
        rows = pl.ds(pl.multiple_of(at * RANK, RANK), RANK)
        total = lax.dot_general(c_ref[0, rows], rhs[0], NT, preferred_element_type=jnp.float32)
        total += lax.dot_general(c_ref[1, rows], rhs[1], NT, preferred_element_type=jnp.float32)
        o_ref[...] = total.astype(jnp.bfloat16)


def early_kernel(hops, own_ref, got_ref, *refs):
    half = own_ref.shape[0]
    arrived, c_ref, outs, rhs = refs[: half - 1], refs[half - 1], refs[half:-1], refs[-1]
    row = lax.axis_index("row")
    for k in range(2 * half):
        at = pl.ds(pl.multiple_of((row ^ k) * RANK, RANK), RANK)
        if k < 2:
            value = (own_ref, got_ref)[k][0]
        else:
            value = arrived[k // 2 - 1][k % 2]
        rhs[0, :, at] = value
        rhs[1, :, at] = turn_rows(value)
    couple(hops, c_ref, rhs, outs)


def late_kernel(hops, rhs, c_ref, *outs):
    couple(hops, c_ref, rhs, outs)


def mid(kernel, hops, operands, coupling, extra):
    width = operands[0].shape[1]
    share = len(hops) * RANK * coupling.shape[2]
    return pl.pallas_call(
        functools.partial(kernel, hops),
        out_shape=[jax.ShapeDtypeStruct((RANK, width), jnp.bfloat16)] * len(hops) + extra,
        in_specs=[VMEM] * (len(operands) + 1),
        out_specs=[VMEM] * (len(hops) + len(extra)),
        compiler_params=params(4),
        cost_estimate=cost(4 * width * share, share * 4),
        name="mid",
    )(*operands, coupling)


def far_kernel(hops, *refs):
    landed, (u_ref, n_ref, o_ref, data) = refs[: len(hops)], refs[len(hops) :]
    me = lax.axis_index("col")
    for n, k in enumerate(hops):
        at = pl.ds(pl.multiple_of((n & ~1) * RANK + ((me ^ k) & 1) * RANK, RANK), RANK)
        value = landed[n][...]
        data[0, at] = value
        data[1, at] = turn_lanes(value.astype(jnp.float32)).astype(jnp.bfloat16)
    step = 2 * RANK
    for i in range(0, n_ref.shape[0], step):
        rows = slice(i, i + step)
        total = n_ref[rows]
        for n in range(0, len(hops), 2):
            lanes = pl.ds(pl.multiple_of(((me ^ hops[n]) & ~1) * RANK, 2 * RANK), 2 * RANK)
            at = slice(n * RANK, (n + 2) * RANK)
            total += dot(u_ref[0, rows, lanes], data[0, at]) + dot(u_ref[1, rows, lanes], data[1, at])
        o_ref[rows] = total.astype(o_ref.dtype)


def far(hops, landed, factors, near_field, kind):
    count, width = near_field.shape
    share = len(hops) * RANK * count
    return pl.pallas_call(
        functools.partial(far_kernel, hops),
        out_shape=jax.ShapeDtypeStruct((count, width), kind),
        in_specs=[VMEM] * (len(hops) + 2),
        out_specs=VMEM,
        scratch_shapes=[pltpu.VMEM((2, len(hops) * RANK, width), jnp.bfloat16)],
        compiler_params=params(4),
        cost_estimate=cost(4 * width * share, share * 4),
        name="far",
    )(*landed, factors, near_field)


def stages(excitation, near_list, near_blocks, col_factors, coupling, row_factors):
    row_count = lax.axis_size("row")
    col_count = lax.axis_size("col")
    total = row_count * col_count
    axes = ("row", "col")
    inner = [(i, i ^ 1) for i in range(total)]
    outer, edge = [], []
    for i in range(1, total - 1):
        j = ((i + 1) ^ 1) - 1
        (outer if i // col_count == j // col_count else edge).append((i, j))
    third = lax.ppermute(excitation, axes, edge)
    second = lax.ppermute(excitation, axes, outer)
    first = lax.ppermute(excitation, axes, inner)
    own, cross = project(excitation, col_factors)
    steps = row_count // 2
    beyond, close = list(range(steps // 2, steps)), list(range(1, steps // 2))
    aside = [(i, i ^ 1) for i in range(row_count)]
    got_beyond = lax.ppermute(cross[steps // 2 :], "row", aside)
    got = lax.ppermute(cross[: steps // 2], "row", aside)
    sent = dict(zip(beyond, pack(beyond, own, got_beyond)))
    sent.update(zip(close, pack(close, own, got)))
    arrived = []
    for k in range(1, steps):
        arrived.append(lax.ppermute(sent[k], "row", [(i, i ^ (2 * k)) for i in range(row_count)]))
    slots = slots_of(near_list)
    table = table_of(excitation, first)
    early = list(range(2, col_count))
    late = [1, 0]
    turned = jax.ShapeDtypeStruct((2, own.shape[1], coupling.shape[2]), own.dtype)
    *blocks, rhs = mid(early_kernel, early, [own, got, *arrived], coupling, [turned])
    sent = dict(zip(early, blocks))
    sent.update(zip(late, mid(late_kernel, late, [rhs], coupling, [])))
    landed = {0: sent[0]}
    for k in reversed(range(1, col_count)):
        landed[k] = lax.ppermute(sent[k], "col", [(i, i ^ k) for i in range(col_count)])
    total = near(slots, table, second, third, near_blocks)
    total = far([0, 1], [landed[0], landed[1]], row_factors, total, jnp.float32)
    return far(early, [landed[k] for k in early], row_factors, total, jnp.bfloat16)


def solution(mesh):
    return jax.shard_map(
        stages,
        mesh=mesh,
        in_specs=(
            P(("row", "col"), None),
            P(("row", "col"), None),
            P(None, ("row", "col"), None),
            P(None, ("row", "col"), None),
            P(None, ("row", "col"), None),
            P(None, ("row", "col"), None),
        ),
        out_specs=P(("row", "col"), None),
        check_vma=False,
    )
```

```python
import functools

import jax
import jax.numpy as jnp
from jax import lax
from jax.experimental import pallas as pl
from jax.experimental.pallas import tpu as pltpu
from jax.sharding import PartitionSpec as P

RANK = 128
LEAF = 128
NEAR = 5
MIB = 1 << 20
VMEM = pl.BlockSpec(memory_space=pltpu.VMEM)
HBM = pl.BlockSpec(memory_space=pltpu.HBM)
SMEM = pl.BlockSpec(memory_space=pltpu.SMEM)
NT = (((1,), (1,)), ((), ()))


def params(mib):
    return pltpu.CompilerParams(vmem_limit_bytes=int(mib * MIB))


def cost(flops, moved):
    return pl.CostEstimate(flops=flops, bytes_accessed=moved, transcendentals=0)


def dot(a, b):
    return jnp.dot(a, b, preferred_element_type=jnp.float32)


def turn_rows(v):
    half = v.shape[0] // 2
    return jnp.concatenate([-v[half:], v[:half]], axis=0)


def turn_lanes(v):
    half = v.shape[-1] // 2
    rolled = pltpu.roll(v, half, v.ndim - 1)
    lane = lax.broadcasted_iota(jnp.int32, v.shape, v.ndim - 1)
    return jnp.where(lane < half, -rolled, rolled)


def project_kernel(x_hbm, v_hbm, own_ref, cross_ref, x_ref, v_ref, lhs, part, x_sem, v_sem):
    row = lax.axis_index("row")
    half = x_ref.shape[0] // 2
    wide = 2 * RANK
    pieces = v_ref.shape[2] // wide

    def fetch(k, p):
        rows = pl.ds(k * half, half)
        return pltpu.make_async_copy(v_hbm.at[p, rows], v_ref.at[p, rows], v_sem.at[k, p])

    def product(k, n):
        rows = slice(k * half, (k + 1) * half)
        lanes = slice(n * wide, (n + 1) * wide)
        return dot(lhs[0, :, rows], v_ref[0, rows, lanes]) + dot(lhs[1, :, rows], v_ref[1, rows, lanes])

    load = pltpu.make_async_copy(x_hbm, x_ref, x_sem)
    load.start()
    for k in range(2):
        for p in range(2):
            fetch(k, p).start()
    load.wait()
    turned = x_ref[...].astype(jnp.float32).T.astype(jnp.bfloat16)
    lhs[0] = turned
    lhs[1] = turn_rows(turned)
    for p in range(2):
        fetch(0, p).wait()
    for n in range(pieces):
        part[n] = product(0, n)
    for p in range(2):
        fetch(1, p).wait()
    for n in range(pieces):
        total = (part[n] + product(1, n)).astype(jnp.bfloat16)
        first, second = total[:, :RANK], total[:, RANK:]
        at = n ^ (row // 2)
        own_ref[at] = jnp.where(row % 2 == 0, first, second)
        cross_ref[at] = jnp.where(row % 2 == 0, second, first)


def project(x, v):
    groups = v.shape[2] // RANK
    count, width = x.shape
    return pl.pallas_call(
        project_kernel,
        out_shape=[jax.ShapeDtypeStruct((groups // 2, width, RANK), jnp.bfloat16)] * 2,
        in_specs=[HBM, HBM],
        out_specs=[VMEM, VMEM],
        scratch_shapes=[
            pltpu.VMEM(x.shape, x.dtype),
            pltpu.VMEM(v.shape, v.dtype),
            pltpu.VMEM((2, width, count), v.dtype),
            pltpu.VMEM((groups // 2, width, 2 * RANK), jnp.float32),
            pltpu.SemaphoreType.DMA(()),
            pltpu.SemaphoreType.DMA((2, 2)),
        ],
        compiler_params=params(53.6),
        cost_estimate=cost(4 * width * v.shape[1] * v.shape[2], v.size * 2),
        name="project",
    )(x, v)


def slots_kernel(list_ref, o_ref):
    leaves = list_ref.shape[0]
    here = lax.axis_index(("row", "col"))
    odd = lax.rem(here, 2)
    at = list_ref[...] - here * leaves
    below = at + leaves * jnp.where(odd == 1, 2, 3)
    above = at + leaves * jnp.where(odd == 1, 1, 0)
    o_ref[...] = jnp.where(at < 0, below, jnp.where(at >= leaves, above, at))


def slots_of(near_list):
    return pl.pallas_call(
        slots_kernel,
        out_shape=jax.ShapeDtypeStruct(near_list.shape, jnp.int32),
        in_specs=[VMEM],
        out_specs=VMEM,
        compiler_params=params(1),
        cost_estimate=cost(10**10, near_list.size * 8),
        name="slots",
    )(near_list)


def table_kernel(own_ref, first_ref, o_ref):
    count = own_ref.shape[0]
    o_ref[:count] = own_ref[...]
    o_ref[count : 2 * count] = first_ref[...]


def table_of(own, first):
    count, width = own.shape
    return pl.pallas_call(
        table_kernel,
        out_shape=jax.ShapeDtypeStruct((3 * count, width), own.dtype),
        in_specs=[VMEM, VMEM],
        out_specs=VMEM,
        compiler_params=params(1),
        cost_estimate=cost(0, own.size * 8),
        name="table",
    )(own, first)


def awaits_edge():
    col = lax.axis_index("col")
    here = lax.axis_index(("row", "col"))
    last = lax.axis_size("row") * lax.axis_size("col") - 1
    edge = (col == 0) | (col == lax.axis_size("col") - 1)
    return edge & (here != 0) & (here != last)


def near_kernel(late, slot_ref, table_in, side_ref, p_ref, *refs):
    o_ref, table, rhs = refs[-3:]
    count = side_ref.shape[0]

    @pl.when(awaits_edge() == late)
    def _():
        table[2 * count :] = side_ref[...]
        slots = slot_ref[...] * LEAF
        for i in range(count // LEAF):
            rows = slice(i * LEAF, (i + 1) * LEAF)
            for j in range(NEAR):
                at = pl.ds(pl.multiple_of(slots[i, j], LEAF), LEAF)
                rhs[i % 2, j * LEAF : (j + 1) * LEAF] = table[at]
            data = rhs[i % 2]
            straight = dot(p_ref[0, rows], data)
            crossed = dot(p_ref[1, rows], data)
            o_ref[rows] = straight + turn_lanes(crossed)


def near(late, slots, table, side, blocks, *total):
    count, width = side.shape
    return pl.pallas_call(
        functools.partial(near_kernel, late),
        out_shape=[
            jax.ShapeDtypeStruct((count, width), jnp.float32),
            jax.ShapeDtypeStruct(table.shape, table.dtype),
        ],
        in_specs=[VMEM] * (4 + len(total)),
        out_specs=[VMEM, VMEM],
        input_output_aliases={1: 1, 4: 0} if total else {1: 1},
        scratch_shapes=[pltpu.VMEM((2, NEAR * LEAF, width), jnp.bfloat16)],
        compiler_params=params(4),
        cost_estimate=cost(4 * width * blocks.shape[1] * blocks.shape[2], blocks.size * 2),
        name="blocks",
    )(slots, table, side, blocks, *total)


def pack_kernel(own_ref, got_ref, *outs):
    for k, o_ref in enumerate(outs):
        o_ref[0] = own_ref[k + 1]
        o_ref[1] = got_ref[k + 1]


def pack(own, got):
    count = own.shape[0] - 1
    return pl.pallas_call(
        pack_kernel,
        out_shape=[jax.ShapeDtypeStruct((2, *own.shape[1:]), own.dtype)] * count,
        in_specs=[VMEM, VMEM],
        out_specs=[VMEM] * count,
        compiler_params=params(1),
        cost_estimate=cost(0, own.size * 8),
        name="pack",
    )(own, got)


def couple(hops, c_ref, rhs, outs):
    for k, o_ref in zip(hops, outs):
        at = lax.axis_index("col") ^ k
        rows = pl.ds(pl.multiple_of(at * RANK, RANK), RANK)
        total = lax.dot_general(c_ref[0, rows], rhs[0], NT, preferred_element_type=jnp.float32)
        total += lax.dot_general(c_ref[1, rows], rhs[1], NT, preferred_element_type=jnp.float32)
        o_ref[...] = total.astype(jnp.bfloat16)


def early_kernel(hops, own_ref, got_ref, *refs):
    half = own_ref.shape[0]
    arrived, c_ref, outs, rhs = refs[: half - 1], refs[half - 1], refs[half:-1], refs[-1]
    row = lax.axis_index("row")
    for k in range(2 * half):
        at = pl.ds(pl.multiple_of((row ^ k) * RANK, RANK), RANK)
        if k < 2:
            value = (own_ref, got_ref)[k][0]
        else:
            value = arrived[k // 2 - 1][k % 2]
        rhs[0, :, at] = value
        rhs[1, :, at] = turn_rows(value)
    couple(hops, c_ref, rhs, outs)


def late_kernel(hops, rhs, c_ref, *outs):
    couple(hops, c_ref, rhs, outs)


def mid(kernel, hops, operands, coupling, extra):
    width = operands[0].shape[1]
    share = len(hops) * RANK * coupling.shape[2]
    return pl.pallas_call(
        functools.partial(kernel, hops),
        out_shape=[jax.ShapeDtypeStruct((RANK, width), jnp.bfloat16)] * len(hops) + extra,
        in_specs=[VMEM] * (len(operands) + 1),
        out_specs=[VMEM] * (len(hops) + len(extra)),
        compiler_params=params(4),
        cost_estimate=cost(4 * width * share, share * 4),
        name="mid",
    )(*operands, coupling)


def far_kernel(hops, *refs):
    landed, u_ref, addends, (o_ref, data) = refs[: len(hops)], refs[len(hops)], refs[len(hops) + 1 : -2], refs[-2:]
    me = lax.axis_index("col")
    for n, k in enumerate(hops):
        at = pl.ds(pl.multiple_of((n & ~1) * RANK + ((me ^ k) & 1) * RANK, RANK), RANK)
        value = landed[n][...]
        data[0, at] = value
        data[1, at] = turn_lanes(value.astype(jnp.float32)).astype(jnp.bfloat16)
    step = 2 * RANK
    for i in range(0, o_ref.shape[0], step):
        rows = slice(i, i + step)
        terms = [ref[rows] for ref in addends]
        for n in range(0, len(hops), 2):
            lanes = pl.ds(pl.multiple_of(((me ^ hops[n]) & ~1) * RANK, 2 * RANK), 2 * RANK)
            at = slice(n * RANK, (n + 2) * RANK)
            terms.append(dot(u_ref[0, rows, lanes], data[0, at]) + dot(u_ref[1, rows, lanes], data[1, at]))
        o_ref[rows] = sum(terms[1:], terms[0]).astype(o_ref.dtype)


def far(hops, landed, factors, addends, kind):
    count, width = factors.shape[1], landed[0].shape[1]
    share = len(hops) * RANK * count
    return pl.pallas_call(
        functools.partial(far_kernel, hops),
        out_shape=jax.ShapeDtypeStruct((count, width), kind),
        in_specs=[VMEM] * (len(hops) + 1 + len(addends)),
        out_specs=VMEM,
        scratch_shapes=[pltpu.VMEM((2, len(hops) * RANK, width), jnp.bfloat16)],
        compiler_params=params(4),
        cost_estimate=cost(4 * width * share, share * 4),
        name="far",
    )(*landed, factors, *addends)


def stages(excitation, near_list, near_blocks, col_factors, coupling, row_factors):
    row_count = lax.axis_size("row")
    col_count = lax.axis_size("col")
    total = row_count * col_count
    axes = ("row", "col")
    inner = [(i, i ^ 1) for i in range(total)]
    outer, edge = [], []
    for i in range(1, total - 1):
        j = ((i + 1) ^ 1) - 1
        (outer if i // col_count == j // col_count else edge).append((i, j))
    third = lax.ppermute(excitation, axes, edge)
    second = lax.ppermute(excitation, axes, outer)
    first = lax.ppermute(excitation, axes, inner)
    own, cross = project(excitation, col_factors)
    got = lax.ppermute(cross, "row", [(i, i ^ 1) for i in range(row_count)])
    sent = pack(own, got)
    arrived = []
    for k in range(1, row_count // 2):
        arrived.append(lax.ppermute(sent[k - 1], "row", [(i, i ^ (2 * k)) for i in range(row_count)]))
    slots = slots_of(near_list)
    table = table_of(excitation, first)
    total, table = near(False, slots, table, second, near_blocks)
    early = list(range(2, col_count))
    late = [1, 0]
    turned = jax.ShapeDtypeStruct((2, own.shape[1], coupling.shape[2]), own.dtype)
    *blocks, rhs = mid(early_kernel, early, [own, got, *arrived], coupling, [turned])
    sent = dict(zip(early, blocks))
    sent.update(zip(late, mid(late_kernel, late, [rhs], coupling, [])))
    landed = {0: sent[0]}
    for k in reversed(range(1, col_count)):
        landed[k] = lax.ppermute(sent[k], "col", [(i, i ^ k) for i in range(col_count)])
    partial = far([0, 1], [landed[0], landed[1]], row_factors, [], jnp.float32)
    total, _ = near(True, slots, table, third, near_blocks, total)
    return far(early, [landed[k] for k in early], row_factors, [partial, total], jnp.bfloat16)


def solution(mesh):
    return jax.shard_map(
        stages,
        mesh=mesh,
        in_specs=(
            P(("row", "col"), None),
            P(("row", "col"), None),
            P(None, ("row", "col"), None),
            P(None, ("row", "col"), None),
            P(None, ("row", "col"), None),
            P(None, ("row", "col"), None),
        ),
        out_specs=P(("row", "col"), None),
        check_vma=False,
    )
```
